32 devices in a mesh: dp: 8 (over z, x), tensor: 4 (over y, core).
Axes of the slice: x: 2, y: 2, z: 4, core: 2. Of those that a mesh axis runs over, the one named last changes fastest.
Arguments:
- grads: bfloat16 [8, 2, 48, 256, 1024], P('dp', None, None, None, 'tensor'), may hold values from -70 to 70
- owner: int32 [48], replicated, may hold values from 0 to 7, as said below
- master: float32 [96, 256, 1024], P('dp', None, 'tensor'), may hold values from -0.1875 to 0.1875
- moment1: float32 [96, 256, 1024], P('dp', None, 'tensor'), may hold values from -2 to 2
- moment2: float32 [96, 256, 1024], P('dp', None, 'tensor'), may hold values from 0.01 to 1
Outputs:
- master_new: float32 [96, 256, 1024], P('dp', None, 'tensor')
- moment1_new: float32 [96, 256, 1024], P('dp', None, 'tensor')
- moment2_new: float32 [96, 256, 1024], P('dp', None, 'tensor')
- weights: bfloat16 [48, 256, 1024], P(None, None, 'tensor')
- norm_ratio: float32 [], replicated
The draws below stay inside these ranges and needn't reach their ends.
Inputs may be any that keep to these rules, and one draw needn't show every extreme that they name: `owner`: no data index owns more than 12 groups, one owns exactly 12, and the first and the last index own at least one.
All inputs are finite; a program needn't handle non-finite values.
Results may differ from the reference program's by a relative error of at most 0.005.
Values may be sent and summed in bfloat16 or wider, within the bound.
A program may use at most 192 MiB of HBM per device.

```python
import math
import jax
import jax.numpy as jnp
from jax import lax

D = 1024
ROWS = 256
GROUPS = 48
SLOTS = 12
N_DP = 8


def draw_grads(key, part):
    key_noise, key_group, key_col = jax.random.split(key, 3)
    shape = (N_DP, 2, GROUPS, ROWS, D)
    group_scale = jax.random.uniform(key_group, (GROUPS,), jnp.float32, jnp.log(0.3), jnp.log(3.0))
    group_scale = jnp.exp(group_scale)
    column = jnp.arange(D, dtype=jnp.float32)
    col_rise = 1.0 + 2.0 * column / (D - 1)
    col_scale = col_rise * jnp.exp(jax.random.uniform(key_col, (D,), jnp.float32, jnp.log(0.6), jnp.log(1.6)))
    scale = group_scale[None, None, :, None, None] * col_scale[None, None, None, None, :]
    values = jnp.clip(jax.random.normal(key_noise, shape, jnp.float32), -4.0, 4.0)
    return (values * scale).astype(jnp.bfloat16)


def draw_owner(key, part):
    key_perm, key_full, key_order = jax.random.split(jax.random.fold_in(key, 17), 3)
    total = N_DP * SLOTS
    perm = jax.random.permutation(key_perm, total)
    ranks = jnp.argsort(perm).astype(jnp.int32)
    full_owner = jax.random.randint(key_full, (), 0, N_DP)
    posn = jnp.arange(total, dtype=jnp.int32)
    forced = (posn // SLOTS == full_owner) | (posn == 0) | (posn == (N_DP - 1) * SLOTS)
    score = jnp.where(forced, ranks - 2 * total, ranks)
    chosen = jnp.argsort(score)[:GROUPS].astype(jnp.int32)
    chosen = chosen[jax.random.permutation(key_order, GROUPS)]
    return (chosen // SLOTS).astype(jnp.int32)


def level_of(stream_key, dims, pieces, least, top_value):
    def one(position, parts):
        steps = jax.random.uniform(jax.random.fold_in(jax.random.fold_in(stream_key, 6), position), (parts,), jnp.float32, least / len(pieces), top_value / len(pieces))
        return jnp.repeat(jnp.exp(steps), dims[position] // parts).reshape((-1,) + (1,) * (len(dims) - position - 1))

    gain = one(*pieces[0])
    for cut in pieces[1:]:
        gain = gain * one(*cut)
    return gain


def normal_values(key, dims, scale, most, pieces=(), held_as=jnp.bfloat16):
    array = jax.random.normal(key, dims, jnp.float32) * scale
    if len(pieces) > 0:
        array = level_of(key, dims, pieces, -0.22, 0.18) * array
    return jnp.clip(array, min=-most, max=most).astype(held_as)


def setup_inputs(seed: int = 0) -> dict:
    splits = jax.random.split(jax.random.key(seed), 6)
    grads = draw_grads(jax.random.fold_in(splits[5], 71), 0)
    owner = draw_owner(jax.random.fold_in(splits[5], 71), 0)
    master = normal_values(splits[2], (N_DP * SLOTS, ROWS, D), D ** -0.5, 0.1875, ((0, 8), (2, 4)), jnp.float32)
    moment1 = normal_values(splits[3], (N_DP * SLOTS, ROWS, D), 0.3, 2.0, ((0, 8), (2, 4)), jnp.float32)
    moment2 = jnp.clip(jnp.exp(math.log(1.0) - 4.6051702 * jax.random.uniform(splits[4], (N_DP * SLOTS, ROWS, D), jnp.float32) ** level_of(splits[4], (N_DP * SLOTS, ROWS, D), ((0, 8), (2, 4)), -0.2, 0.2)), 0.01, 1.0)
    return {"grads": grads, "owner": owner, "master": master, "moment1": moment1, "moment2": moment2}


beta_one = 0.9
beta_two = 0.98
learn_rate = 0.004
weight_decay = 0.01
adam_eps = 1e-06
step_count = 100

def slot_positions(owner, slot_count):
    count = owner.shape[0]
    same = owner[:, None] == owner[None, :]
    earlier = jnp.arange(count, dtype=jnp.int32)[:, None] > jnp.arange(count, dtype=jnp.int32)[None, :]
    order_in = lax.optimization_barrier(jnp.sum((same & earlier).astype(jnp.int32), axis=1)).astype(jnp.int32)
    return (owner * slot_count + order_in).astype(jnp.int32)

def adam_update(grad, master, moment1, moment2, clip):
    clipped = clip * grad
    first = beta_one * moment1 + (1.0 - beta_one) * clipped
    second = beta_two * moment2 + (1.0 - beta_two) * clipped * clipped
    fix_one = 1.0 - beta_one ** step_count
    fix_two = 1.0 - beta_two ** step_count
    update = first / fix_one / (jnp.sqrt(second / fix_two) + adam_eps) + weight_decay * master
    return (master - learn_rate * update, first, second)

def reference(grads, owner, master, moment1, moment2):

    def add_replica(total, replica):
        return (total + replica[0].astype(jnp.float32) + replica[1].astype(jnp.float32), None)
    start = jnp.zeros((GROUPS, ROWS, D), jnp.float32)
    grad_sum, _ = lax.scan(add_replica, start, grads)
    slot_pos = slot_positions(owner, SLOTS)
    slots_all = N_DP * SLOTS
    matches = slot_pos[None, :] == jnp.arange(slots_all, dtype=jnp.int32)[:, None]
    group_ids = lax.optimization_barrier(jnp.sum(matches.astype(jnp.int32) * jnp.arange(GROUPS, dtype=jnp.int32)[None, :], axis=1)).astype(jnp.int32)
    used = jnp.any(matches, axis=1)
    slot_grad = jnp.take(grad_sum, group_ids, axis=0) * used[:, None, None].astype(jnp.float32)
    total = jnp.sum(slot_grad * slot_grad)
    bound = math.sqrt(GROUPS * ROWS * D)
    norm_value = jnp.sqrt(total)
    norm_ratio = norm_value / bound
    clip = bound / jnp.maximum(norm_value, bound)
    master_new, moment1_new, moment2_new = adam_update(slot_grad, master, moment1, moment2, clip)
    weights = jnp.take(master_new, slot_pos, axis=0).astype(jnp.bfloat16)
    return (master_new, moment1_new, moment2_new, weights, norm_ratio)
```

```python
import functools
import math

import jax
import jax.numpy as jnp
from jax import lax
from jax.experimental import pallas as pl
from jax.experimental.pallas import tpu as pltpu
from jax.sharding import PartitionSpec as P

D = 1024
ROWS = 256
GROUPS = 48


beta_one = 0.9
beta_two = 0.98
learn_rate = 0.004
weight_decay = 0.01
adam_eps = 1e-06
step_count = 100


def order_within(owner):
    count = owner.shape[0]
    same = owner[:, None] == owner[None, :]
    earlier = (
        jnp.arange(count, dtype=jnp.int32)[:, None] > jnp.arange(count, dtype=jnp.int32)[None, :]
    )
    return jnp.sum((same & earlier).astype(jnp.int32), axis=1)


def adam_update(grad, master, moment1, moment2, clip):
    clipped = clip * grad
    first = beta_one * moment1 + (1.0 - beta_one) * clipped
    second = beta_two * moment2 + (1.0 - beta_two) * clipped * clipped
    fix_one = 1.0 - beta_one**step_count
    fix_two = 1.0 - beta_two**step_count
    update = first / fix_one / (jnp.sqrt(second / fix_two) + adam_eps) + weight_decay * master
    return (master - learn_rate * update, first, second)


Z = 4
X = 2
MESH = pl.DeviceIdType.MESH
F32 = jnp.float32
BF16 = jnp.bfloat16


def place():
    me = lax.axis_index("dp")
    return lax.div(me, X), lax.rem(me, X), lax.axis_index("tensor")


def barrier(z, x, tensor, lanes):
    sem = pltpu.get_barrier_semaphore()
    pl.semaphore_signal(sem, inc=1, device_id={"dp": z * X + 1 - x}, device_id_type=MESH)
    for step in range(1, Z):
        other = lax.rem(z + step, Z)
        pl.semaphore_signal(sem, inc=1, device_id={"dp": other * X + x}, device_id_type=MESH)
    if lanes > 1:
        for step in range(1, lanes):
            other = lax.rem(tensor + step, lanes)
            pl.semaphore_signal(sem, inc=1, device_id={"tensor": other}, device_id_type=MESH)
    pl.semaphore_wait(sem, Z + lanes - 1)


def reduce_kernel(
    n, lanes, ids_ref, used_ref, grads_ref, out_ref, total_ref,
    held, xsend, xrecv, acc, rrecv, lrecv, norm1, norm2, norm3,
    hsem, xs, xr, rs, rr, ls, lr, ns, nr,
):
    z, x, tensor = place()
    rows = acc.shape[2]
    part = 64
    load = pltpu.make_async_copy(grads_ref, held, hsem)
    load.start()
    barrier(z, x, tensor, lanes)
    load.wait()

    def x_copy(k):
        return pltpu.make_async_remote_copy(
            src_ref=xsend.at[k], dst_ref=xrecv.at[k], send_sem=xs.at[k], recv_sem=xr.at[k],
            device_id={"dp": z * X + 1 - x}, device_id_type=MESH)

    def right_copy(k, d):
        return pltpu.make_async_remote_copy(
            src_ref=acc.at[k, d], dst_ref=rrecv.at[k, d], send_sem=rs.at[k, d], recv_sem=rr.at[k, d],
            device_id={"dp": lax.rem(z + 1, Z) * X + x}, device_id_type=MESH)

    def left_copy(k, d):
        return pltpu.make_async_remote_copy(
            src_ref=acc.at[k, d], dst_ref=lrecv.at[k, d], send_sem=ls.at[k, d], recv_sem=lr.at[k, d],
            device_id={"dp": lax.rem(z + Z - 1, Z) * X + x}, device_id_type=MESH)

    def local(k, col, d, span):
        i = (k * X + col) * Z + d
        g = ids_ref[i]
        return (held[0, g, span].astype(F32) + held[1, g, span].astype(F32)) * used_ref[i]

    def build(k):
        for d in range(Z):
            def body(j, c, d=d):
                span = pl.ds(pl.multiple_of(j * part, part), part)
                xsend[k, d, span] = local(k, 1 - x, d, span).astype(BF16)
                return c
            lax.fori_loop(0, rows // part, body, 0)
        x_copy(k).start()

    ahead = min(3, n)
    for k in range(ahead):
        build(k)

    def tick(t, carry):
        @pl.when(t + ahead < n)
        def _():
            build(t + ahead)

        @pl.when(t < n)
        def _():
            x_copy(t).wait_recv()
            for d in range(Z):
                def body(j, c, d=d):
                    span = pl.ds(pl.multiple_of(j * part, part), part)
                    acc[t, d, span] = (local(t, x, d, span) + xrecv[t, d, span].astype(F32)).astype(BF16)
                    return c
                lax.fori_loop(0, rows // part, body, 0)

        def stage(k, first, last, recv, copy, beyond):
            @pl.when((k >= 0) & (k < n))
            def _():
                for d in range(Z):
                    @pl.when(beyond(d))
                    def _(d=d):
                        @pl.when(jnp.logical_not(first))
                        def _():
                            copy(k, d).wait_recv()
                            def body(j, c):
                                span = pl.ds(pl.multiple_of(j * part, part), part)
                                acc[k, d, span] = (acc[k, d, span].astype(F32) + recv[k, d, span].astype(F32)).astype(BF16)
                                return c
                            lax.fori_loop(0, rows // part, body, 0)
                        copy(k, d).start()

        stage(t - z, z == 0, z == Z - 1, rrecv, right_copy, lambda d: d > z)
        stage(t - (Z - 1 - z), z == Z - 1, z == 0, lrecv, left_copy, lambda d: d < z)

        k = t - (Z - 1)
        @pl.when(k >= 0)
        def _():
            def first(j, c):
                span = pl.ds(pl.multiple_of(j * part, part), part)
                out_ref[k, span] = acc[k, z, span].astype(F32)
                return c
            lax.fori_loop(0, rows // part, first, 0)
            for edge, copy, recv in ((0, right_copy, rrecv), (Z - 1, left_copy, lrecv)):
                @pl.when(z != edge)
                def _(copy=copy, recv=recv):
                    copy(k, z).wait_recv()
                    def body(j, c):
                        span = pl.ds(pl.multiple_of(j * part, part), part)
                        out_ref[k, span] = out_ref[k, span] + recv[k, z, span].astype(F32)
                        return c
                    lax.fori_loop(0, rows // part, body, 0)

        return carry

    lax.fori_loop(0, n + Z - 1, tick, 0)

    width = out_ref.shape[2]
    def squares(j, c):
        k, j = lax.div(j, rows // part), lax.rem(j, rows // part)
        v = out_ref[k, pl.ds(pl.multiple_of(j * part, part), part)]
        v = jnp.sum((v * v).reshape(part // 8, 8, width), axis=0)
        for m in range(width // 128):
            c = c + v[:, m * 128:(m + 1) * 128]
        return c
    own = lax.fori_loop(0, n * (rows // part), squares, jnp.zeros((8, 128), F32))

    def share(buf, mine, count, base, target):
        def copy(slot, step, device):
            return pltpu.make_async_remote_copy(
                src_ref=buf.at[mine], dst_ref=buf.at[slot], send_sem=ns.at[base + step],
                recv_sem=nr.at[base + step], device_id=device, device_id_type=MESH)
        for step in range(1, count):
            copy(mine, step, target(step)).start()
        for step in range(1, count):
            came = lax.rem(mine + count - step, count)
            copy(came, step, target(step)).wait()
        value = buf[0]
        for i in range(1, count):
            value = value + buf[i]
        return value

    norm1[x] = own
    value = share(norm1, x, X, 0, lambda s: {"dp": z * X + lax.rem(x + s, X)})
    norm2[z] = value
    value = share(norm2, z, Z, X, lambda s: {"dp": lax.rem(z + s, Z) * X + x})
    norm3[tensor] = value
    value = share(norm3, tensor, lanes, X + Z, lambda s: {"tensor": lax.rem(tensor + s, lanes)})
    total_ref[...] = value

    def finish(k, carry):
        x_copy(k).wait_send()
        for d in range(Z):
            @pl.when(d > z)
            def _(d=d):
                right_copy(k, d).wait_send()
            @pl.when(d < z)
            def _(d=d):
                left_copy(k, d).wait_send()
        return carry

    lax.fori_loop(0, n, finish, 0)


def reduce_slots(n, lanes, number, ids, used, grads):
    _, groups, rows, width = grads.shape
    block = (rows, width)
    return pl.pallas_call(
        functools.partial(reduce_kernel, n, lanes),
        out_shape=(
            jax.ShapeDtypeStruct((n,) + block, F32),
            jax.ShapeDtypeStruct((8, 128), F32),
        ),
        in_specs=[
            pl.BlockSpec(memory_space=pltpu.SMEM),
            pl.BlockSpec(memory_space=pltpu.SMEM),
            pl.BlockSpec(memory_space=pl.ANY),
        ],
        out_specs=(pl.BlockSpec(memory_space=pltpu.VMEM), pl.BlockSpec(memory_space=pltpu.VMEM)),
        scratch_shapes=[
            pltpu.VMEM((2, groups) + block, BF16),
            pltpu.VMEM((n, Z) + block, BF16),
            pltpu.VMEM((n, Z) + block, BF16),
            pltpu.VMEM((n, Z) + block, BF16),
            pltpu.VMEM((n, Z) + block, BF16),
            pltpu.VMEM((n, Z) + block, BF16),
            pltpu.VMEM((X, 8, 128), F32),
            pltpu.VMEM((Z, 8, 128), F32),
            pltpu.VMEM((lanes, 8, 128), F32),
            pltpu.SemaphoreType.DMA,
            pltpu.SemaphoreType.DMA((n,)),
            pltpu.SemaphoreType.DMA((n,)),
            pltpu.SemaphoreType.DMA((n, Z)),
            pltpu.SemaphoreType.DMA((n, Z)),
            pltpu.SemaphoreType.DMA((n, Z)),
            pltpu.SemaphoreType.DMA((n, Z)),
            pltpu.SemaphoreType.DMA((X + Z + lanes,)),
            pltpu.SemaphoreType.DMA((X + Z + lanes,)),
        ],
        compiler_params=pltpu.CompilerParams(
            collective_id=number, has_side_effects=True, vmem_limit_bytes=60 * 2**20
        ),
    )(ids, used, grads)


def gather_kernel(n, fresh_ref, out_ref, osem, xs, xr, rs, ls, zr):
    z, x, tensor = place()
    barrier(z, x, tensor, 1)

    def x_copy(src, k, d, col):
        return pltpu.make_async_remote_copy(
            src_ref=src, dst_ref=out_ref.at[k, col, d], send_sem=xs.at[k, d], recv_sem=xr.at[k, d],
            device_id={"dp": z * X + 1 - x}, device_id_type=MESH)

    def line_copy(src, k, d, step, sems):
        return pltpu.make_async_remote_copy(
            src_ref=src, dst_ref=out_ref.at[k, x, d], send_sem=sems.at[k, d], recv_sem=zr.at[k, d],
            device_id={"dp": lax.rem(z + Z + step, Z) * X + x}, device_id_type=MESH)

    def own_copy(k):
        return pltpu.make_async_copy(fresh_ref.at[k], out_ref.at[k, x, z], osem.at[k])

    def tick(t, carry):
        @pl.when(t < n)
        def _():
            @pl.when(z < Z - 1)
            def _():
                line_copy(fresh_ref.at[t], t, z, 1, rs).start()
            @pl.when(z > 0)
            def _():
                line_copy(fresh_ref.at[t], t, z, -1, ls).start()
            x_copy(fresh_ref.at[t], t, z, x).start()
            own_copy(t).start()
        for hop in range(1, Z):
            k = t - hop
            @pl.when((k >= 0) & (k < n))
            def _(k=k, hop=hop):
                for d, step, sems, here, more in (
                    (z - hop, 1, rs, z - hop >= 0, z < Z - 1),
                    (z + hop, -1, ls, z + hop < Z, z > 0),
                ):
                    @pl.when(here)
                    def _(d=d, step=step, sems=sems, more=more):
                        block = out_ref.at[k, x, d]
                        line_copy(block, k, d, step, sems).wait_recv()
                        @pl.when(more)
                        def _():
                            line_copy(block, k, d, step, sems).start()
                        x_copy(block, k, d, x).start()
        return carry

    lax.fori_loop(0, n + Z - 1, tick, 0)

    def finish(k, carry):
        own_copy(k).wait()
        for d in range(Z):
            x_copy(out_ref.at[k, x, d], k, d, x).wait_send()
            x_copy(out_ref.at[k, x, d], k, d, 1 - x).wait_recv()
            @pl.when((d <= z) & (z < Z - 1))
            def _(d=d):
                line_copy(out_ref.at[k, x, d], k, d, 1, rs).wait_send()
            @pl.when((d >= z) & (z > 0))
            def _(d=d):
                line_copy(out_ref.at[k, x, d], k, d, -1, ls).wait_send()
        return carry

    lax.fori_loop(0, n, finish, 0)


def gather_slots(number, fresh):
    n = fresh.shape[0]
    return pl.pallas_call(
        functools.partial(gather_kernel, n),
        out_shape=jax.ShapeDtypeStruct((n, X, Z) + fresh.shape[1:], BF16),
        in_specs=[pl.BlockSpec(memory_space=pl.ANY)],
        out_specs=pl.BlockSpec(memory_space=pl.ANY),
        scratch_shapes=[pltpu.SemaphoreType.DMA((n,))] + [pltpu.SemaphoreType.DMA((n, Z))] * 5,
        compiler_params=pltpu.CompilerParams(collective_id=number, has_side_effects=True),
    )(fresh)


def pick_kernel(pos_ref, slots_ref, out_ref, sems):
    count = out_ref.shape[0]

    def copy(g):
        return pltpu.make_async_copy(slots_ref.at[pos_ref[g]], out_ref.at[g], sems.at[g])

    def start(g, c):
        copy(g).start()
        return c

    def done(g, c):
        copy(g).wait()
        return c

    lax.fori_loop(0, count, start, 0)
    lax.fori_loop(0, count, done, 0)


def pick(pos, slots):
    count = pos.shape[0]
    return pl.pallas_call(
        pick_kernel,
        out_shape=jax.ShapeDtypeStruct((count,) + slots.shape[1:], slots.dtype),
        in_specs=[pl.BlockSpec(memory_space=pltpu.SMEM), pl.BlockSpec(memory_space=pl.ANY)],
        out_specs=pl.BlockSpec(memory_space=pl.ANY),
        scratch_shapes=[pltpu.SemaphoreType.DMA((count,))],
    )(pos, slots)


def lookup(pos, slots_all):
    matches = pos[None, :] == jnp.arange(slots_all, dtype=jnp.int32)[:, None]
    ids = jnp.sum(
        matches.astype(jnp.int32) * jnp.arange(pos.shape[0], dtype=jnp.int32)[None, :], axis=1
    )
    return ids, jnp.any(matches, axis=1).astype(F32)


def on_slice(lanes, grads, owner, master, moment1, moment2):
    slots = master.shape[0]
    col, line = lax.rem(owner, X), lax.div(owner, X)
    order_in = order_within(owner)
    pos = (order_in * X + col) * Z + line
    ids, used = lookup(pos, slots * X * Z)
    own_grad, sums = reduce_slots(slots, lanes, 0, ids, used, grads[0])
    total = jnp.sum(sums)
    bound = math.sqrt(GROUPS * ROWS * D)
    norm_value = jnp.sqrt(total)
    norm_ratio = norm_value / bound
    clip = bound / jnp.maximum(norm_value, bound)
    master_new, moment1_new, moment2_new = adam_update(own_grad, master, moment1, moment2, clip)
    every = gather_slots(1, master_new.astype(BF16))
    weights = pick(pos, every.reshape((slots * X * Z,) + master.shape[1:]))
    return (master_new, moment1_new, moment2_new, weights, norm_ratio)


def on_device(grads, owner, master, moment1, moment2):
    slot_count = master.shape[0]
    owners_all = lax.axis_size("dp")
    slots_all = owners_all * slot_count
    group_count = owner.shape[0]
    summed = grads[0, 0].astype(jnp.float32) + grads[0, 1].astype(jnp.float32)
    order_in = order_within(owner)
    slot_pos = owner * slot_count + order_in
    matches = slot_pos[None, :] == jnp.arange(slots_all, dtype=jnp.int32)[:, None]
    group_ids = jnp.sum(
        matches.astype(jnp.int32) * jnp.arange(group_count, dtype=jnp.int32)[None, :], axis=1
    )
    used = jnp.any(matches, axis=1).astype(jnp.float32)
    own_grad = lax.psum_scatter(
        (jnp.take(summed, group_ids, axis=0) * used[:, None, None]).astype(jnp.bfloat16),
        "dp",
        scatter_dimension=0,
        tiled=True,
    ).astype(jnp.float32)
    total = lax.psum(jnp.sum(own_grad * own_grad), ("dp", "tensor"))
    bound = math.sqrt(GROUPS * ROWS * D)
    norm_value = jnp.sqrt(total)
    norm_ratio = norm_value / bound
    clip = bound / jnp.maximum(norm_value, bound)
    master_new, moment1_new, moment2_new = adam_update(own_grad, master, moment1, moment2, clip)
    fresh = master_new.astype(jnp.bfloat16)
    every_slot = lax.all_gather(fresh, "dp", axis=0, tiled=True)
    weights = jnp.take(every_slot, slot_pos, axis=0)
    return (master_new, moment1_new, moment2_new, weights, norm_ratio)


def solution(mesh):
    body = on_device
    if mesh.shape["dp"] == Z * X:
        body = functools.partial(on_slice, mesh.shape["tensor"])
    return jax.shard_map(
        body,
        mesh=mesh,
        in_specs=(
            P("dp", None, None, None, "tensor"),
            P(),
            P("dp", None, "tensor"),
            P("dp", None, "tensor"),
            P("dp", None, "tensor"),
        ),
        out_specs=(
            P("dp", None, "tensor"),
            P("dp", None, "tensor"),
            P("dp", None, "tensor"),
            P(None, None, "tensor"),
            P(),
        ),
        check_vma=False,
    )
```

```python
import functools
import math

import jax
import jax.numpy as jnp
from jax import lax
from jax.experimental import pallas as pl
from jax.experimental.pallas import tpu as pltpu
from jax.sharding import PartitionSpec as P

D = 1024
ROWS = 256
GROUPS = 48


beta_one = 0.9
beta_two = 0.98
learn_rate = 0.004
weight_decay = 0.01
adam_eps = 1e-06
step_count = 100


def order_within(owner):
    count = owner.shape[0]
    same = owner[:, None] == owner[None, :]
    earlier = (
        jnp.arange(count, dtype=jnp.int32)[:, None] > jnp.arange(count, dtype=jnp.int32)[None, :]
    )
    return jnp.sum((same & earlier).astype(jnp.int32), axis=1)


def adam_update(grad, master, moment1, moment2, clip):
    clipped = clip * grad
    first = beta_one * moment1 + (1.0 - beta_one) * clipped
    second = beta_two * moment2 + (1.0 - beta_two) * clipped * clipped
    fix_one = 1.0 - beta_one**step_count
    fix_two = 1.0 - beta_two**step_count
    update = first / fix_one / (jnp.sqrt(second / fix_two) + adam_eps) + weight_decay * master
    return (master - learn_rate * update, first, second)


Z = 4
X = 2
MESH = pl.DeviceIdType.MESH
F32 = jnp.float32
BF16 = jnp.bfloat16


def place():
    me = lax.axis_index("dp")
    return lax.div(me, X), lax.rem(me, X), lax.axis_index("tensor")


def barrier(z, x, tensor, lanes):
    sem = pltpu.get_barrier_semaphore()
    pl.semaphore_signal(sem, inc=1, device_id={"dp": z * X + 1 - x}, device_id_type=MESH)
    for step in range(1, Z):
        other = lax.rem(z + step, Z)
        pl.semaphore_signal(sem, inc=1, device_id={"dp": other * X + x}, device_id_type=MESH)
    if lanes > 1:
        for step in range(1, lanes):
            other = lax.rem(tensor + step, lanes)
            pl.semaphore_signal(sem, inc=1, device_id={"tensor": other}, device_id_type=MESH)
    pl.semaphore_wait(sem, Z + lanes - 1)


def spread(z, x, out, xs, xr, rs, ls, zr):
    def x_copy(src, k, d, col):
        at = col * Z + d
        return pltpu.make_async_remote_copy(
            src_ref=src, dst_ref=out.at[k, at], send_sem=xs.at[k, d], recv_sem=xr.at[k, d],
            device_id={"dp": z * X + 1 - x}, device_id_type=MESH)

    def line_copy(src, k, d, step, sems):
        return pltpu.make_async_remote_copy(
            src_ref=src, dst_ref=out.at[k, x * Z + d], send_sem=sems.at[k, d], recv_sem=zr.at[k, d],
            device_id={"dp": lax.rem(z + Z + step, Z) * X + x}, device_id_type=MESH)

    def begin(src, k):
        @pl.when(z < Z - 1)
        def _():
            line_copy(src, k, z, 1, rs).start()
        @pl.when(z > 0)
        def _():
            line_copy(src, k, z, -1, ls).start()
        x_copy(src, k, z, x).start()

    def forward(k, hop):
        for d, step, sems, here, more in (
            (z - hop, 1, rs, z - hop >= 0, z < Z - 1),
            (z + hop, -1, ls, z + hop < Z, z > 0),
        ):
            @pl.when(here)
            def _(d=d, step=step, sems=sems, more=more):
                block = out.at[k, x * Z + d]
                line_copy(block, k, d, step, sems).wait_recv()
                @pl.when(more)
                def _():
                    line_copy(block, k, d, step, sems).start()
                x_copy(block, k, d, x).start()

    def arrived(k):
        for d in range(Z):
            x_copy(out.at[k, x * Z + d], k, d, 1 - x).wait_recv()

    def sent(k):
        for d in range(Z):
            x_copy(out.at[k, x * Z + d], k, d, x).wait_send()
            @pl.when((d <= z) & (z < Z - 1))
            def _(d=d):
                line_copy(out.at[k, x * Z + d], k, d, 1, rs).wait_send()
            @pl.when((d >= z) & (z > 0))
            def _(d=d):
                line_copy(out.at[k, x * Z + d], k, d, -1, ls).wait_send()

    return begin, forward, arrived, sent


def rows_loop(rows, body, part=64):
    def one(j, c):
        body(pl.ds(pl.multiple_of(j * part, part), part))
        return c
    lax.fori_loop(0, rows // part, one, 0)


def scatter(z, x, local, xsend, xrecv, acc, rrecv, lrecv, xs, xr, rs, rr, ls, lr):
    rows = acc.shape[2]

    def x_copy(k):
        return pltpu.make_async_remote_copy(
            src_ref=xsend.at[k], dst_ref=xrecv.at[k], send_sem=xs.at[k], recv_sem=xr.at[k],
            device_id={"dp": z * X + 1 - x}, device_id_type=MESH)

    def right_copy(k, d):
        return pltpu.make_async_remote_copy(
            src_ref=acc.at[k, d], dst_ref=rrecv.at[k, d], send_sem=rs.at[k, d], recv_sem=rr.at[k, d],
            device_id={"dp": lax.rem(z + 1, Z) * X + x}, device_id_type=MESH)

    def left_copy(k, d):
        return pltpu.make_async_remote_copy(
            src_ref=acc.at[k, d], dst_ref=lrecv.at[k, d], send_sem=ls.at[k, d], recv_sem=lr.at[k, d],
            device_id={"dp": lax.rem(z + Z - 1, Z) * X + x}, device_id_type=MESH)

    def build(k):
        for d in range(Z):
            def body(span, d=d):
                xsend[k, d, span] = local(k, 1 - x, d, span).astype(BF16)
            rows_loop(rows, body)
        x_copy(k).start()

    def pair(k):
        x_copy(k).wait_recv()
        for d in range(Z):
            def body(span, d=d):
                acc[k, d, span] = (local(k, x, d, span) + xrecv[k, d, span].astype(F32)).astype(BF16)
            rows_loop(rows, body)

    def stage(k, first, recv, copy, beyond, order):
        for d in order:
            @pl.when(beyond(d))
            def _(d=d):
                @pl.when(jnp.logical_not(first))
                def _():
                    copy(k, d).wait_recv()
                    def body(span):
                        acc[k, d, span] = (acc[k, d, span].astype(F32) + recv[k, d, span].astype(F32)).astype(BF16)
                    rows_loop(rows, body)
                copy(k, d).start()

    def right(k):
        stage(k, z == 0, rrecv, right_copy, lambda d: d > z, range(Z - 1, -1, -1))

    def left(k):
        stage(k, z == Z - 1, lrecv, left_copy, lambda d: d < z, range(Z))

    def final(k, out, row):
        def first(span):
            out[row, span] = acc[k, z, span].astype(F32)
        rows_loop(rows, first)
        for edge, copy, recv in ((0, right_copy, rrecv), (Z - 1, left_copy, lrecv)):
            @pl.when(z != edge)
            def _(copy=copy, recv=recv):
                copy(k, z).wait_recv()
                def body(span):
                    out[row, span] = out[row, span] + recv[k, z, span].astype(F32)
                rows_loop(rows, body)

    def sent(k):
        x_copy(k).wait_send()
        for d in range(Z):
            @pl.when(d > z)
            def _(d=d):
                right_copy(k, d).wait_send()
            @pl.when(d < z)
            def _(d=d):
                left_copy(k, d).wait_send()

    return build, pair, right, left, final, sent


def when_in(k, n, f):
    @pl.when((k >= 0) & (k < n))
    def _():
        f(k)


def reduce_kernel(n, lanes, extra, *refs):
    if extra:
        ids_ref, used_ref, eids_ref, eused_ref, grads_ref, out_ref, total_ref, shared, *refs = refs
        esems, refs = refs[:5], refs[5:]
    else:
        ids_ref, used_ref, grads_ref, out_ref, total_ref, *refs = refs
    held, norm1, norm2, norm3, hsem, ns, nr, *work = refs
    z, x, tensor = place()
    slots, rows, width = out_ref.shape
    part = 64
    load = pltpu.make_async_copy(grads_ref, held, hsem)
    load.start()
    barrier(z, x, tensor, lanes)
    load.wait()

    def local(k, col, d, span):
        i = (k * X + col) * Z + d
        g = ids_ref[i]
        return (held[0, g, span].astype(F32) + held[1, g, span].astype(F32)) * used_ref[i]

    build, pair, right, left, final, sent = scatter(z, x, local, *work)
    if extra:
        begin, forward, arrived, gone = spread(z, x, shared, *esems)

    def row_of(k):
        return lax.rem(k - extra + slots, slots)

    ahead = min(3, n)
    for k in range(ahead):
        build(k)

    def tick(t, carry):
        when_in(t + ahead, n, build)
        when_in(t, n, pair)
        when_in(t - z, n, right)
        when_in(t - (Z - 1 - z), n, left)
        when_in(t - (Z - 1), n, lambda k: final(k, out_ref, row_of(k)))
        if extra:
            @pl.when(t == Z - 1)
            def _():
                def body(span):
                    shared[0, x * Z + z, span] = out_ref[slots - 1, span].astype(BF16)
                rows_loop(rows, body)
                begin(shared.at[0, x * Z + z], 0)
            for hop in range(1, Z):
                @pl.when(t == Z - 1 + 2 * hop)
                def _(hop=hop):
                    forward(0, hop)
        return carry

    lax.fori_loop(0, n + Z - 1, tick, 0)

    def squares(j, c):
        k, j = lax.div(j, rows // part), lax.rem(j, rows // part)
        v = out_ref[row_of(k), pl.ds(pl.multiple_of(j * part, part), part)]
        v = jnp.sum((v * v).reshape(part // 8, 8, width), axis=0)
        for m in range(width // 128):
            c = c + v[:, m * 128:(m + 1) * 128]
        return c
    own = lax.fori_loop(0, n * (rows // part), squares, jnp.zeros((8, 128), F32))

    def share(buf, mine, count, base, target):
        def copy(slot, step, device):
            return pltpu.make_async_remote_copy(
                src_ref=buf.at[mine], dst_ref=buf.at[slot], send_sem=ns.at[base + step],
                recv_sem=nr.at[base + step], device_id=device, device_id_type=MESH)
        for step in range(1, count):
            copy(mine, step, target(step)).start()
        for step in range(1, count):
            came = lax.rem(mine + count - step, count)
            copy(came, step, target(step)).wait()
        value = buf[0]
        for i in range(1, count):
            value = value + buf[i]
        return value

    norm1[x] = own
    value = share(norm1, x, X, 0, lambda s: {"dp": z * X + lax.rem(x + s, X)})
    norm2[z] = value
    value = share(norm2, z, Z, X, lambda s: {"dp": lax.rem(z + s, Z) * X + x})
    norm3[tensor] = value
    value = share(norm3, tensor, lanes, X + Z, lambda s: {"tensor": lax.rem(tensor + s, lanes)})
    total_ref[...] = value

    if extra:
        arrived(0)
        for s in range(n - 1, slots):
            i = s - (n - 1)
            def body(span, s=s, i=i):
                out_ref[s, span] = shared[0, eids_ref[i], span].astype(F32) * eused_ref[i]
            rows_loop(rows, body)
        gone(0)

    def finish(k, carry):
        sent(k)
        return carry

    lax.fori_loop(0, n, finish, 0)


def work_shapes(n, block):
    return [pltpu.VMEM((n, Z) + block, BF16)] * 5 + [
        pltpu.SemaphoreType.DMA((n,)),
        pltpu.SemaphoreType.DMA((n,)),
    ] + [pltpu.SemaphoreType.DMA((n, Z))] * 4


def reduce_slots(n, slots, lanes, number, tables, grads):
    _, groups, rows, width = grads.shape
    block = (rows, width)
    extra = 1 if n < slots else 0
    more = []
    if extra:
        more = [pltpu.VMEM((1, X * Z) + block, BF16)] + [pltpu.SemaphoreType.DMA((1, Z))] * 5
    return pl.pallas_call(
        functools.partial(reduce_kernel, n, lanes, extra),
        out_shape=(
            jax.ShapeDtypeStruct((slots,) + block, F32),
            jax.ShapeDtypeStruct((8, 128), F32),
        ),
        in_specs=[pl.BlockSpec(memory_space=pltpu.SMEM)] * len(tables)
        + [pl.BlockSpec(memory_space=pl.ANY)],
        out_specs=(pl.BlockSpec(memory_space=pltpu.VMEM), pl.BlockSpec(memory_space=pltpu.VMEM)),
        scratch_shapes=more + [
            pltpu.VMEM((2, groups) + block, BF16),
            pltpu.VMEM((X, 8, 128), F32),
            pltpu.VMEM((Z, 8, 128), F32),
            pltpu.VMEM((lanes, 8, 128), F32),
            pltpu.SemaphoreType.DMA,
            pltpu.SemaphoreType.DMA((X + Z + lanes,)),
            pltpu.SemaphoreType.DMA((X + Z + lanes,)),
        ] + work_shapes(n, block),
        compiler_params=pltpu.CompilerParams(
            collective_id=number, has_side_effects=True, vmem_limit_bytes=60 * 2**20
        ),
    )(*tables, grads)


def gather_kernel(n, extra, *refs):
    if extra:
        sids_ref, mine_ref, *refs = refs
    fresh_ref, out_ref, osem, *refs = refs
    esems, refs = refs[:5], refs[5:]
    z, x, tensor = place()
    slots, rows, width = fresh_ref.shape
    plain = n - extra
    barrier(z, x, tensor, 1)
    begin, forward, arrived, gone = spread(z, x, out_ref, *esems)
    if extra:
        summed, mixed, *work = refs

        def local(k, col, d, span):
            i = col * Z + d
            return fresh_ref[sids_ref[i], span].astype(F32) * mine_ref[i]

        build, pair, right, left, final, sent = scatter(z, x, local, *work)
        build(0)

    def own_copy(src, k):
        return pltpu.make_async_copy(src, out_ref.at[k, x * Z + z], osem.at[k])

    def tick(t, carry):
        @pl.when(t < plain)
        def _():
            begin(fresh_ref.at[t], t)
            own_copy(fresh_ref.at[t], t).start()
        if extra:
            @pl.when(t == 1)
            def _():
                pair(0)
            @pl.when(t == 1 + z)
            def _():
                right(0)
            @pl.when(t == Z - z)
            def _():
                left(0)
            @pl.when(t == Z + 1)
            def _():
                final(0, summed, 0)
                def body(span):
                    mixed[0, span] = summed[0, span].astype(BF16)
                rows_loop(rows, body)
            @pl.when(t == plain)
            def _():
                begin(mixed.at[0], plain)
                own_copy(mixed.at[0], plain).start()
        for hop in range(1, Z):
            when_in(t - hop, n, lambda k, hop=hop: forward(k, hop))
        return carry

    lax.fori_loop(0, n + Z - 1, tick, 0)

    def finish(k, carry):
        own_copy(fresh_ref.at[0], k).wait()
        arrived(k)
        gone(k)
        return carry

    lax.fori_loop(0, n, finish, 0)
    if extra:
        sent(0)


def gather_slots(n, number, tables, fresh):
    slots, rows, width = fresh.shape
    block = (rows, width)
    extra = 1 if n < slots else 0
    more = []
    if extra:
        more = [pltpu.VMEM((1,) + block, F32), pltpu.VMEM((1,) + block, BF16)] + work_shapes(1, block)
    return pl.pallas_call(
        functools.partial(gather_kernel, n, extra),
        out_shape=jax.ShapeDtypeStruct((n, X * Z) + block, BF16),
        in_specs=[pl.BlockSpec(memory_space=pltpu.SMEM)] * len(tables)
        + [pl.BlockSpec(memory_space=pltpu.VMEM)],
        out_specs=pl.BlockSpec(memory_space=pl.ANY),
        scratch_shapes=[pltpu.SemaphoreType.DMA((n,))]
        + [pltpu.SemaphoreType.DMA((n, Z))] * 5 + more,
        compiler_params=pltpu.CompilerParams(
            collective_id=number, has_side_effects=True, vmem_limit_bytes=32 * 2**20
        ),
    )(*tables, fresh)


def pick_kernel(pos_ref, *refs):
    out_ref = refs[-1]
    for i, ref in enumerate(refs[:-1]):
        out_ref[i] = ref[0]


def pick(pos, slots):
    count = pos.shape[0]
    rows, width = slots.shape[1:]
    wide = math.gcd(count, 8)
    return pl.pallas_call(
        pick_kernel,
        out_shape=jax.ShapeDtypeStruct((count, rows, width), slots.dtype),
        grid_spec=pltpu.PrefetchScalarGridSpec(
            num_scalar_prefetch=1,
            grid=(count // wide,),
            in_specs=[
                pl.BlockSpec((1, rows, width), lambda i, p, j=j: (p[i * wide + j], 0, 0))
                for j in range(wide)
            ],
            out_specs=pl.BlockSpec((wide, rows, width), lambda i, p: (i, 0, 0)),
        ),
    )(pos, *([slots] * wide))


def lookup(pos, slots_all):
    matches = pos[None, :] == jnp.arange(slots_all, dtype=jnp.int32)[:, None]
    ids = jnp.sum(
        matches.astype(jnp.int32) * jnp.arange(pos.shape[0], dtype=jnp.int32)[None, :], axis=1
    )
    return ids, jnp.any(matches, axis=1).astype(F32)


REGULAR = 7


def on_slice(lanes, grads, owner, master, moment1, moment2):
    slots = master.shape[0]
    count = owner.shape[0]
    own_count = X * Z
    me = lax.axis_index("dp")
    col, line = lax.rem(owner, X), lax.div(owner, X)
    order_in = order_within(owner)
    regular = (order_in * X + col) * Z + line

    over = order_in >= REGULAR
    before = jnp.arange(count)[None, :] < jnp.arange(count)[:, None]
    shared = jnp.sum((over[None, :] & before).astype(jnp.int32), axis=1)
    fits = jnp.sum(over.astype(jnp.int32)) <= own_count

    def few_reduce(part):
        pos = jnp.where(over, shared, own_count + regular)
        ids, used = lookup(pos, (REGULAR + 1) * own_count)
        wanted = jnp.arange(REGULAR, slots, dtype=jnp.int32)
        hit = (owner[None, :] == me) & (order_in[None, :] == wanted[:, None])
        eids = jnp.sum(hit.astype(jnp.int32) * jnp.minimum(shared, own_count - 1)[None, :], axis=1)
        eused = jnp.any(hit, axis=1).astype(F32)
        return reduce_slots(REGULAR + 1, slots, lanes, 0, (ids, used, eids, eused), part)

    def all_reduce(part):
        ids, used = lookup(regular, slots * own_count)
        return reduce_slots(slots, slots, lanes, 1, (ids, used), part)

    own_grad, sums = lax.cond(fits, few_reduce, all_reduce, grads[0])
    total = jnp.sum(sums)
    bound = math.sqrt(GROUPS * ROWS * D)
    norm_value = jnp.sqrt(total)
    norm_ratio = norm_value / bound
    clip = bound / jnp.maximum(norm_value, bound)
    master_new, moment1_new, moment2_new = adam_update(own_grad, master, moment1, moment2, clip)

    def few_gather(fresh):
        place_of = jnp.arange(own_count, dtype=jnp.int32)
        hit = over[None, :] & (shared[None, :] == place_of[:, None]) & (owner[None, :] == me)
        sids = jnp.sum(hit.astype(jnp.int32) * order_in[None, :], axis=1)
        mine = jnp.any(hit, axis=1).astype(F32)
        every = gather_slots(REGULAR + 1, 2, (sids, mine), fresh)
        pos = jnp.where(over, REGULAR * own_count + jnp.minimum(shared, own_count - 1), regular)
        return pick(pos, every.reshape((-1,) + fresh.shape[1:]))

    def all_gather(fresh):
        every = gather_slots(slots, 3, (), fresh)
        return pick(regular, every.reshape((-1,) + fresh.shape[1:]))

    weights = lax.cond(fits, few_gather, all_gather, master_new.astype(BF16))
    return (master_new, moment1_new, moment2_new, weights, norm_ratio)


def on_device(grads, owner, master, moment1, moment2):
    slot_count = master.shape[0]
    owners_all = lax.axis_size("dp")
    slots_all = owners_all * slot_count
    group_count = owner.shape[0]
    summed = grads[0, 0].astype(jnp.float32) + grads[0, 1].astype(jnp.float32)
    order_in = order_within(owner)
    slot_pos = owner * slot_count + order_in
    matches = slot_pos[None, :] == jnp.arange(slots_all, dtype=jnp.int32)[:, None]
    group_ids = jnp.sum(
        matches.astype(jnp.int32) * jnp.arange(group_count, dtype=jnp.int32)[None, :], axis=1
    )
    used = jnp.any(matches, axis=1).astype(jnp.float32)
    own_grad = lax.psum_scatter(
        (jnp.take(summed, group_ids, axis=0) * used[:, None, None]).astype(jnp.bfloat16),
        "dp",
        scatter_dimension=0,
        tiled=True,
    ).astype(jnp.float32)
    total = lax.psum(jnp.sum(own_grad * own_grad), ("dp", "tensor"))
    bound = math.sqrt(GROUPS * ROWS * D)
    norm_value = jnp.sqrt(total)
    norm_ratio = norm_value / bound
    clip = bound / jnp.maximum(norm_value, bound)
    master_new, moment1_new, moment2_new = adam_update(own_grad, master, moment1, moment2, clip)
    fresh = master_new.astype(jnp.bfloat16)
    every_slot = lax.all_gather(fresh, "dp", axis=0, tiled=True)
    weights = jnp.take(every_slot, slot_pos, axis=0)
    return (master_new, moment1_new, moment2_new, weights, norm_ratio)


def solution(mesh):
    body = on_device
    if mesh.shape["dp"] == Z * X:
        body = functools.partial(on_slice, mesh.shape["tensor"])
    return jax.shard_map(
        body,
        mesh=mesh,
        in_specs=(
            P("dp", None, None, None, "tensor"),
            P(),
            P("dp", None, "tensor"),
            P("dp", None, "tensor"),
            P("dp", None, "tensor"),
        ),
        out_specs=(
            P("dp", None, "tensor"),
            P("dp", None, "tensor"),
            P("dp", None, "tensor"),
            P(None, None, "tensor"),
            P(),
        ),
        check_vma=False,
    )
```

```python
import functools
import math

import jax
import jax.numpy as jnp
from jax import lax
from jax.experimental import pallas as pl
from jax.experimental.pallas import tpu as pltpu
from jax.sharding import PartitionSpec as P

D = 1024
ROWS = 256
GROUPS = 48


beta_one = 0.9
beta_two = 0.98
learn_rate = 0.004
weight_decay = 0.01
adam_eps = 1e-06
step_count = 100


def order_within(owner):
    count = owner.shape[0]
    same = owner[:, None] == owner[None, :]
    earlier = (
        jnp.arange(count, dtype=jnp.int32)[:, None] > jnp.arange(count, dtype=jnp.int32)[None, :]
    )
    return jnp.sum((same & earlier).astype(jnp.int32), axis=1)


def adam_update(grad, master, moment1, moment2, clip):
    clipped = clip * grad
    first = beta_one * moment1 + (1.0 - beta_one) * clipped
    second = beta_two * moment2 + (1.0 - beta_two) * clipped * clipped
    fix_one = 1.0 - beta_one**step_count
    fix_two = 1.0 - beta_two**step_count
    update = first / fix_one / (jnp.sqrt(second / fix_two) + adam_eps) + weight_decay * master
    return (master - learn_rate * update, first, second)


Z = 4
X = 2
MESH = pl.DeviceIdType.MESH
F32 = jnp.float32
BF16 = jnp.bfloat16


def place():
    me = lax.axis_index("dp")
    return lax.div(me, X), lax.rem(me, X), lax.axis_index("tensor")


def barrier(z, x, tensor, lanes):
    sem = pltpu.get_barrier_semaphore()
    pl.semaphore_signal(sem, inc=1, device_id={"dp": z * X + 1 - x}, device_id_type=MESH)
    for step in range(1, Z):
        other = lax.rem(z + step, Z)
        pl.semaphore_signal(sem, inc=1, device_id={"dp": other * X + x}, device_id_type=MESH)
    if lanes > 1:
        for step in range(1, lanes):
            other = lax.rem(tensor + step, lanes)
            pl.semaphore_signal(sem, inc=1, device_id={"tensor": other}, device_id_type=MESH)
    pl.semaphore_wait(sem, Z + lanes - 1)


def spread(z, x, out, xs, xr, rs, ls, zr):
    def x_copy(src, k, d, col):
        at = col * Z + d
        return pltpu.make_async_remote_copy(
            src_ref=src, dst_ref=out.at[k, at], send_sem=xs.at[k, d], recv_sem=xr.at[k, d],
            device_id={"dp": z * X + 1 - x}, device_id_type=MESH)

    def line_copy(src, k, d, step, sems):
        return pltpu.make_async_remote_copy(
            src_ref=src, dst_ref=out.at[k, x * Z + d], send_sem=sems.at[k, d], recv_sem=zr.at[k, d],
            device_id={"dp": lax.rem(z + Z + step, Z) * X + x}, device_id_type=MESH)

    def begin(src, k):
        @pl.when(z < Z - 1)
        def _():
            line_copy(src, k, z, 1, rs).start()
        @pl.when(z > 0)
        def _():
            line_copy(src, k, z, -1, ls).start()
        x_copy(src, k, z, x).start()

    def forward(k, hop, across=True):
        for d, step, sems, here, more in (
            (z - hop, 1, rs, z - hop >= 0, z < Z - 1),
            (z + hop, -1, ls, z + hop < Z, z > 0),
        ):
            @pl.when(here)
            def _(d=d, step=step, sems=sems, more=more):
                block = out.at[k, x * Z + d]
                line_copy(block, k, d, step, sems).wait_recv()
                @pl.when(more)
                def _():
                    line_copy(block, k, d, step, sems).start()
                if across:
                    x_copy(block, k, d, x).start()

    def arrived(k, lines=range(Z)):
        for d in lines:
            x_copy(out.at[k, x * Z + d], k, d, 1 - x).wait_recv()

    def sent(k, lines=range(Z)):
        for d in lines:
            x_copy(out.at[k, x * Z + d], k, d, x).wait_send()
        for d in range(Z):
            @pl.when((d <= z) & (z < Z - 1))
            def _(d=d):
                line_copy(out.at[k, x * Z + d], k, d, 1, rs).wait_send()
            @pl.when((d >= z) & (z > 0))
            def _(d=d):
                line_copy(out.at[k, x * Z + d], k, d, -1, ls).wait_send()

    return begin, forward, arrived, sent


def rows_loop(rows, body, part=64):
    def one(j, c):
        body(pl.ds(pl.multiple_of(j * part, part), part))
        return c
    lax.fori_loop(0, rows // part, one, 0)


def scatter(z, x, local, xsend, xrecv, acc, rrecv, lrecv, xs, xr, rs, rr, ls, lr):
    rows = acc.shape[2]

    def x_copy(k):
        return pltpu.make_async_remote_copy(
            src_ref=xsend.at[k], dst_ref=xrecv.at[k], send_sem=xs.at[k], recv_sem=xr.at[k],
            device_id={"dp": z * X + 1 - x}, device_id_type=MESH)

    def right_copy(k, d):
        return pltpu.make_async_remote_copy(
            src_ref=acc.at[k, d], dst_ref=rrecv.at[k, d], send_sem=rs.at[k, d], recv_sem=rr.at[k, d],
            device_id={"dp": lax.rem(z + 1, Z) * X + x}, device_id_type=MESH)

    def left_copy(k, d):
        return pltpu.make_async_remote_copy(
            src_ref=acc.at[k, d], dst_ref=lrecv.at[k, d], send_sem=ls.at[k, d], recv_sem=lr.at[k, d],
            device_id={"dp": lax.rem(z + Z - 1, Z) * X + x}, device_id_type=MESH)

    def build(k):
        for d in range(Z):
            def body(span, d=d):
                xsend[k, d, span] = local(k, 1 - x, d, span).astype(BF16)
            rows_loop(rows, body)
        x_copy(k).start()

    def pair(k):
        x_copy(k).wait_recv()
        for d in range(Z):
            def body(span, d=d):
                acc[k, d, span] = (local(k, x, d, span) + xrecv[k, d, span].astype(F32)).astype(BF16)
            rows_loop(rows, body)

    def stage(k, first, recv, copy, beyond, order):
        for d in order:
            @pl.when(beyond(d))
            def _(d=d):
                @pl.when(jnp.logical_not(first))
                def _():
                    copy(k, d).wait_recv()
                    def body(span):
                        acc[k, d, span] = (acc[k, d, span].astype(F32) + recv[k, d, span].astype(F32)).astype(BF16)
                    rows_loop(rows, body)
                copy(k, d).start()

    def right(k):
        stage(k, z == 0, rrecv, right_copy, lambda d: d > z, range(Z - 1, -1, -1))

    def left(k):
        stage(k, z == Z - 1, lrecv, left_copy, lambda d: d < z, range(Z))

    def final(k, out, row):
        def first(span):
            out[row, span] = acc[k, z, span].astype(F32)
        rows_loop(rows, first)
        for edge, copy, recv in ((0, right_copy, rrecv), (Z - 1, left_copy, lrecv)):
            @pl.when(z != edge)
            def _(copy=copy, recv=recv):
                copy(k, z).wait_recv()
                def body(span):
                    out[row, span] = out[row, span] + recv[k, z, span].astype(F32)
                rows_loop(rows, body)

    def sent(k):
        if xs is not None:
            x_copy(k).wait_send()
        for d in range(Z):
            @pl.when(d > z)
            def _(d=d):
                right_copy(k, d).wait_send()
            @pl.when(d < z)
            def _(d=d):
                left_copy(k, d).wait_send()

    return build, pair, right, left, final, sent


def when_in(k, n, f):
    @pl.when((k >= 0) & (k < n))
    def _():
        f(k)


def reduce_kernel(n, lanes, extra, *refs):
    if extra:
        ids_ref, used_ref, eids_ref, eused_ref, grads_ref, out_ref, total_ref, shared, *refs = refs
        esems, refs = refs[:5], refs[5:]
    else:
        ids_ref, used_ref, grads_ref, out_ref, total_ref, *refs = refs
    held, norm1, norm2, norm3, hsem, ns, nr, wsum, wsend, wrecv, wx, *refs = refs
    wacc, wright, wleft, wrs, wrr, wls, wlr, *work = refs
    z, x, tensor = place()
    slots, rows, width = out_ref.shape
    last = n - 1
    part = 64
    load = pltpu.make_async_copy(grads_ref, held, hsem)
    load.start()
    barrier(z, x, tensor, lanes)
    load.wait()

    def local(k, col, d, span):
        i = (k * X + col) * Z + d
        g = ids_ref[i]
        return (held[0, g, span].astype(F32) + held[1, g, span].astype(F32)) * used_ref[i]

    build, pair, right, left, final, sent = scatter(z, x, local, *work)
    if extra:
        begin, forward, arrived, gone = spread(z, x, shared, *esems)

    _, _, wide_right, wide_left, wide_final, wide_sent = scatter(
        z, x, local, None, None, wacc, wright, wleft, None, None, wrs, wrr, wls, wlr)

    def row_of(k):
        return lax.rem(k - extra + slots, slots)

    def cross():
        return pltpu.make_async_remote_copy(
            src_ref=wsend, dst_ref=wrecv, send_sem=wx.at[0], recv_sem=wx.at[1],
            device_id={"dp": z * X + 1 - x}, device_id_type=MESH)

    ahead = min(3, last)
    for k in range(ahead):
        build(k)
    for c in range(X):
        for d in range(Z):
            def fill(span, c=c, d=d):
                col = x if c == 0 else 1 - x
                wacc[c, d, span] = local(last, col, d, span).astype(BF16)
            rows_loop(rows, fill)

    def tick(t, carry):
        when_in(t + ahead, last, build)
        @pl.when(t == z)
        def _():
            for c in (1, 0):
                wide_right(c)
        @pl.when(t == Z - 1 - z)
        def _():
            for c in (1, 0):
                wide_left(c)
        when_in(t, last, pair)
        when_in(t - z, last, right)
        when_in(t - (Z - 1 - z), last, left)
        @pl.when(t == Z)
        def _():
            for c in range(X):
                wide_final(c, wsum, c)
            def body(span):
                wsend[span] = wsum[1, span].astype(BF16)
            rows_loop(rows, body)
            cross().start()
        when_in(t - (Z - 1), last, lambda k: final(k, out_ref, row_of(k)))
        if extra:
            @pl.when(t == Z - 1)
            def _():
                def body(span):
                    shared[0, x * Z + z, span] = out_ref[slots - 1, span].astype(BF16)
                rows_loop(rows, body)
                begin(shared.at[0, x * Z + z], 0)
            for hop in range(1, Z):
                @pl.when(t == Z - 1 + 2 * hop)
                def _(hop=hop):
                    forward(0, hop)
        return carry

    lax.fori_loop(0, max(last + Z - 1, 3 * Z - 2), tick, 0)
    cross().wait()
    def add_cross(span):
        out_ref[row_of(last), span] = wsum[0, span] + wrecv[span].astype(F32)
    rows_loop(rows, add_cross)

    def squares(j, c):
        k, j = lax.div(j, rows // part), lax.rem(j, rows // part)
        v = out_ref[row_of(k), pl.ds(pl.multiple_of(j * part, part), part)]
        v = jnp.sum((v * v).reshape(part // 8, 8, width), axis=0)
        for m in range(width // 128):
            c = c + v[:, m * 128:(m + 1) * 128]
        return c
    own = lax.fori_loop(0, n * (rows // part), squares, jnp.zeros((8, 128), F32))

    def share(buf, mine, count, base, target):
        def copy(slot, step, device):
            return pltpu.make_async_remote_copy(
                src_ref=buf.at[mine], dst_ref=buf.at[slot], send_sem=ns.at[base + step],
                recv_sem=nr.at[base + step], device_id=device, device_id_type=MESH)
        for step in range(1, count):
            copy(mine, step, target(step)).start()
        for step in range(1, count):
            came = lax.rem(mine + count - step, count)
            copy(came, step, target(step)).wait()
        value = buf[0]
        for i in range(1, count):
            value = value + buf[i]
        return value

    norm1[x] = own
    value = share(norm1, x, X, 0, lambda s: {"dp": z * X + lax.rem(x + s, X)})
    norm2[z] = value
    value = share(norm2, z, Z, X, lambda s: {"dp": lax.rem(z + s, Z) * X + x})
    norm3[tensor] = value
    value = share(norm3, tensor, lanes, X + Z, lambda s: {"tensor": lax.rem(tensor + s, lanes)})
    total_ref[...] = value

    if extra:
        arrived(0)
        for s in range(n - 1, slots):
            i = s - (n - 1)
            def body(span, s=s, i=i):
                out_ref[s, span] = shared[0, eids_ref[i], span].astype(F32) * eused_ref[i]
            rows_loop(rows, body)
        gone(0)
    for c in range(X):
        wide_sent(c)

    def finish(k, carry):
        sent(k)
        return carry

    lax.fori_loop(0, last, finish, 0)


def work_shapes(n, block):
    return [pltpu.VMEM((n, Z) + block, BF16)] * 5 + [
        pltpu.SemaphoreType.DMA((n,)),
        pltpu.SemaphoreType.DMA((n,)),
    ] + [pltpu.SemaphoreType.DMA((n, Z))] * 4


def reduce_slots(n, slots, lanes, number, tables, grads):
    _, groups, rows, width = grads.shape
    block = (rows, width)
    extra = 1 if n < slots else 0
    more = []
    if extra:
        more = [pltpu.VMEM((1, X * Z) + block, BF16)] + [pltpu.SemaphoreType.DMA((1, Z))] * 5
    return pl.pallas_call(
        functools.partial(reduce_kernel, n, lanes, extra),
        out_shape=(
            jax.ShapeDtypeStruct((slots,) + block, F32),
            jax.ShapeDtypeStruct((8, 128), F32),
        ),
        in_specs=[pl.BlockSpec(memory_space=pltpu.SMEM)] * len(tables)
        + [pl.BlockSpec(memory_space=pl.ANY)],
        out_specs=(pl.BlockSpec(memory_space=pltpu.VMEM), pl.BlockSpec(memory_space=pltpu.VMEM)),
        scratch_shapes=more + [
            pltpu.VMEM((2, groups) + block, BF16),
            pltpu.VMEM((X, 8, 128), F32),
            pltpu.VMEM((Z, 8, 128), F32),
            pltpu.VMEM((lanes, 8, 128), F32),
            pltpu.SemaphoreType.DMA,
            pltpu.SemaphoreType.DMA((X + Z + lanes,)),
            pltpu.SemaphoreType.DMA((X + Z + lanes,)),
            pltpu.VMEM((X,) + block, F32),
            pltpu.VMEM(block, BF16),
            pltpu.VMEM(block, BF16),
            pltpu.SemaphoreType.DMA((2,)),
        ] + [pltpu.VMEM((X, Z) + block, BF16)] * 3
        + [pltpu.SemaphoreType.DMA((X, Z))] * 4 + work_shapes(n - 1, block),
        compiler_params=pltpu.CompilerParams(
            collective_id=number, has_side_effects=True, vmem_limit_bytes=60 * 2**20
        ),
    )(*tables, grads)


def gather_kernel(n, extra, *refs):
    if extra:
        sids_ref, mine_ref, *refs = refs
    fresh_ref, out_ref, osem, *refs = refs
    esems, refs = refs[:5], refs[5:]
    wsems, refs = refs[:3], refs[3:]
    z, x, tensor = place()
    slots, rows, width = fresh_ref.shape
    plain = n - extra
    barrier(z, x, tensor, 1)
    begin, forward, arrived, gone = spread(z, x, out_ref, *esems)
    if extra:
        summed, mixed, *work = refs

        def local(k, col, d, span):
            i = col * Z + d
            return fresh_ref[sids_ref[i], span].astype(F32) * mine_ref[i]

        build, pair, right, left, final, sent = scatter(z, x, local, *work)
        build(0)

    def wide_copy(d, step):
        side = 0 if step > 0 else 1
        block = out_ref.at[0, (1 - x) * Z + d]
        return pltpu.make_async_remote_copy(
            src_ref=block, dst_ref=block, send_sem=wsems[side].at[d], recv_sem=wsems[2].at[d],
            device_id={"dp": lax.rem(z + Z + step, Z) * X + x}, device_id_type=MESH)

    def wide_send(d, step):
        @pl.when((z < Z - 1) if step > 0 else (z > 0))
        def _():
            wide_copy(d, step).start()

    def own_copy(src, k):
        return pltpu.make_async_copy(src, out_ref.at[k, x * Z + z], osem.at[k])

    def tick(t, carry):
        @pl.when(t < plain)
        def _():
            begin(fresh_ref.at[t], t)
            own_copy(fresh_ref.at[t], t).start()
        if extra:
            @pl.when(t == 1)
            def _():
                pair(0)
            @pl.when(t == 1 + z)
            def _():
                right(0)
            @pl.when(t == Z - z)
            def _():
                left(0)
            @pl.when(t == Z + 1)
            def _():
                final(0, summed, 0)
                def body(span):
                    mixed[0, span] = summed[0, span].astype(BF16)
                rows_loop(rows, body)
            @pl.when(t == plain)
            def _():
                begin(mixed.at[0], plain)
                own_copy(mixed.at[0], plain).start()
        @pl.when(t == 1)
        def _():
            arrived(0, (z,))
            wide_send(z, 1)
            wide_send(z, -1)
        for hop in range(1, Z):
            @pl.when(t == hop)
            def _(hop=hop):
                forward(0, hop, False)
            when_in(t - hop - 1, n - 1, lambda k, hop=hop: forward(k + 1, hop))
            @pl.when(t == hop + 1)
            def _(hop=hop):
                for d, step, here in ((z - hop, 1, z - hop >= 0), (z + hop, -1, z + hop < Z)):
                    @pl.when(here)
                    def _(d=d, step=step):
                        wide_copy(d, step).wait_recv()
                        wide_send(d, step)
        return carry

    lax.fori_loop(0, n + Z - 1, tick, 0)

    def finish(k, carry):
        own_copy(fresh_ref.at[0], k).wait()
        arrived(k)
        gone(k)
        return carry

    lax.fori_loop(1, n, finish, 0)
    own_copy(fresh_ref.at[0], 0).wait()
    gone(0, (z,))
    for d in range(Z):
        @pl.when((d <= z) & (z < Z - 1))
        def _(d=d):
            wide_copy(d, 1).wait_send()
        @pl.when((d >= z) & (z > 0))
        def _(d=d):
            wide_copy(d, -1).wait_send()
    if extra:
        sent(0)


def gather_slots(n, number, tables, fresh):
    slots, rows, width = fresh.shape
    block = (rows, width)
    extra = 1 if n < slots else 0
    more = []
    if extra:
        more = [pltpu.VMEM((1,) + block, F32), pltpu.VMEM((1,) + block, BF16)] + work_shapes(1, block)
    return pl.pallas_call(
        functools.partial(gather_kernel, n, extra),
        out_shape=jax.ShapeDtypeStruct((n, X * Z) + block, BF16),
        in_specs=[pl.BlockSpec(memory_space=pltpu.SMEM)] * len(tables)
        + [pl.BlockSpec(memory_space=pltpu.VMEM)],
        out_specs=pl.BlockSpec(memory_space=pl.ANY),
        scratch_shapes=[pltpu.SemaphoreType.DMA((n,))]
        + [pltpu.SemaphoreType.DMA((n, Z))] * 5 + [pltpu.SemaphoreType.DMA((Z,))] * 3 + more,
        compiler_params=pltpu.CompilerParams(
            collective_id=number, has_side_effects=True, vmem_limit_bytes=32 * 2**20
        ),
    )(*tables, fresh)


def pick_kernel(pos_ref, *refs):
    out_ref = refs[-1]
    for i, ref in enumerate(refs[:-1]):
        out_ref[i] = ref[0]


def pick(pos, slots):
    count = pos.shape[0]
    rows, width = slots.shape[1:]
    wide = math.gcd(count, 8)
    return pl.pallas_call(
        pick_kernel,
        out_shape=jax.ShapeDtypeStruct((count, rows, width), slots.dtype),
        grid_spec=pltpu.PrefetchScalarGridSpec(
            num_scalar_prefetch=1,
            grid=(count // wide,),
            in_specs=[
                pl.BlockSpec((1, rows, width), lambda i, p, j=j: (p[i * wide + j], 0, 0))
                for j in range(wide)
            ],
            out_specs=pl.BlockSpec((wide, rows, width), lambda i, p: (i, 0, 0)),
        ),
        compiler_params=pltpu.CompilerParams(vmem_limit_bytes=60 * 2**20),
    )(pos, *([slots] * wide))


def lookup(pos, slots_all):
    matches = pos[None, :] == jnp.arange(slots_all, dtype=jnp.int32)[:, None]
    ids = jnp.sum(
        matches.astype(jnp.int32) * jnp.arange(pos.shape[0], dtype=jnp.int32)[None, :], axis=1
    )
    return ids, jnp.any(matches, axis=1).astype(F32)


CAPACITIES = (6, 7)


def on_slice(lanes, grads, owner, master, moment1, moment2):
    slots = master.shape[0]
    count = owner.shape[0]
    own_count = X * Z
    me = lax.axis_index("dp")
    col, line = lax.rem(owner, X), lax.div(owner, X)
    order_in = order_within(owner)
    regular = (order_in * X + col) * Z + line
    slot_pos = owner * slots + order_in

    def beyond(regulars):
        over = order_in >= regulars
        before = jnp.arange(count)[None, :] < jnp.arange(count)[:, None]
        shared = jnp.sum((over[None, :] & before).astype(jnp.int32), axis=1)
        return over, jnp.minimum(shared, own_count - 1)

    fits = [jnp.sum((order_in >= c).astype(jnp.int32)) <= own_count for c in CAPACITIES]
    form = jnp.where(fits[0], 0, jnp.where(fits[1], 1, 2))

    def few_reduce(regulars, number, part):
        over, shared = beyond(regulars)
        pos = jnp.where(over, shared, own_count + regular)
        ids, used = lookup(pos, (regulars + 1) * own_count)
        wanted = jnp.arange(regulars, slots, dtype=jnp.int32)
        hit = (owner[None, :] == me) & (order_in[None, :] == wanted[:, None])
        eids = jnp.sum(hit.astype(jnp.int32) * shared[None, :], axis=1)
        eused = jnp.any(hit, axis=1).astype(F32)
        return reduce_slots(regulars + 1, slots, lanes, number, (ids, used, eids, eused), part)

    def all_reduce(part):
        summed = part[0].astype(F32) + part[1].astype(F32)
        ids, used = lookup(slot_pos, slots * own_count)
        own = lax.psum_scatter(
            (jnp.take(summed, ids, axis=0) * used[:, None, None]).astype(BF16),
            "dp",
            scatter_dimension=0,
            tiled=True,
        ).astype(F32)
        total = lax.psum(jnp.sum(own * own), ("dp", "tensor"))
        return own, jnp.zeros((8, 128), F32).at[0, 0].set(total)

    own_grad, sums = lax.switch(
        form,
        [functools.partial(few_reduce, c, i) for i, c in enumerate(CAPACITIES)] + [all_reduce],
        grads[0],
    )
    total = jnp.sum(sums)
    bound = math.sqrt(GROUPS * ROWS * D)
    norm_value = jnp.sqrt(total)
    norm_ratio = norm_value / bound
    clip = bound / jnp.maximum(norm_value, bound)
    master_new, moment1_new, moment2_new = adam_update(own_grad, master, moment1, moment2, clip)

    def few_gather(regulars, number, fresh):
        over, shared = beyond(regulars)
        place_of = jnp.arange(own_count, dtype=jnp.int32)
        hit = over[None, :] & (shared[None, :] == place_of[:, None]) & (owner[None, :] == me)
        sids = jnp.sum(hit.astype(jnp.int32) * order_in[None, :], axis=1)
        mine = jnp.any(hit, axis=1).astype(F32)
        every = gather_slots(regulars + 1, number, (sids, mine), fresh)
        pos = jnp.where(over, regulars * own_count + shared, regular)
        return pick(pos, every.reshape((-1,) + fresh.shape[1:]))

    def all_gather(fresh):
        every = lax.all_gather(fresh, "dp", axis=0, tiled=True)
        return jnp.take(every, slot_pos, axis=0)

    weights = lax.switch(
        form,
        [functools.partial(few_gather, c, 2 + i) for i, c in enumerate(CAPACITIES)] + [all_gather],
        master_new.astype(BF16),
    )
    return (master_new, moment1_new, moment2_new, weights, norm_ratio)


def on_device(grads, owner, master, moment1, moment2):
    slot_count = master.shape[0]
    owners_all = lax.axis_size("dp")
    slots_all = owners_all * slot_count
    group_count = owner.shape[0]
    summed = grads[0, 0].astype(jnp.float32) + grads[0, 1].astype(jnp.float32)
    order_in = order_within(owner)
    slot_pos = owner * slot_count + order_in
    matches = slot_pos[None, :] == jnp.arange(slots_all, dtype=jnp.int32)[:, None]
    group_ids = jnp.sum(
        matches.astype(jnp.int32) * jnp.arange(group_count, dtype=jnp.int32)[None, :], axis=1
    )
    used = jnp.any(matches, axis=1).astype(jnp.float32)
    own_grad = lax.psum_scatter(
        (jnp.take(summed, group_ids, axis=0) * used[:, None, None]).astype(jnp.bfloat16),
        "dp",
        scatter_dimension=0,
        tiled=True,
    ).astype(jnp.float32)
    total = lax.psum(jnp.sum(own_grad * own_grad), ("dp", "tensor"))
    bound = math.sqrt(GROUPS * ROWS * D)
    norm_value = jnp.sqrt(total)
    norm_ratio = norm_value / bound
    clip = bound / jnp.maximum(norm_value, bound)
    master_new, moment1_new, moment2_new = adam_update(own_grad, master, moment1, moment2, clip)
    fresh = master_new.astype(jnp.bfloat16)
    every_slot = lax.all_gather(fresh, "dp", axis=0, tiled=True)
    weights = jnp.take(every_slot, slot_pos, axis=0)
    return (master_new, moment1_new, moment2_new, weights, norm_ratio)


def solution(mesh):
    body = on_device
    if mesh.shape["dp"] == Z * X:
        body = functools.partial(on_slice, mesh.shape["tensor"])
    return jax.shard_map(
        body,
        mesh=mesh,
        in_specs=(
            P("dp", None, None, None, "tensor"),
            P(),
            P("dp", None, "tensor"),
            P("dp", None, "tensor"),
            P("dp", None, "tensor"),
        ),
        out_specs=(
            P("dp", None, "tensor"),
            P("dp", None, "tensor"),
            P("dp", None, "tensor"),
            P(None, None, "tensor"),
            P(),
        ),
        check_vma=False,
    )
```
